256 devices in a mesh: walk: 64 (over z, x, core), elec: 2 (over y_lo), chol: 2 (over y_hi).
Axes of the slice: x: 4, y: 4 (y_hi: 2, y_lo: 2; y = y_hi * 2 + y_lo), z: 8, core: 2. Of those that a mesh axis runs over, the one named last changes fastest.
Arguments:
- green: bfloat16 [64, 1024, 256], P('walk'), may hold values from -6 to 6
- chol_vecs: bfloat16 [128, 256, 1024], P(('walk', 'chol'), 'elec'), may hold values from -0.1875 to 0.1875
Outputs:
- gradient: float32 [64, 1024, 256], P('walk', ('elec', 'chol'))
The draws below stay inside these ranges and needn't reach their ends.
All inputs are finite; a program needn't handle non-finite values.
Results may differ from the reference program's by a relative error of at most 0.0029.
Values may be sent and summed in bfloat16 or wider, within the bound.
No kernel may reach another device: no remote copies, remote signals or barrier semaphores. Data moves between devices by JAX's collectives and lax.ppermute only.
A program may use at most 64 MiB of HBM per device.

```python
import jax
import jax.numpy as jnp
from jax import lax

NORB = 1024
NE = 256
NCHOL = 128
NW = 64


def block_scale(key, shape, cuts, low, high):
    level = 1.0
    for axis_at, blocks in cuts:
        steps = jax.random.uniform(jax.random.fold_in(jax.random.fold_in(key, 6), axis_at), (blocks,), jnp.float32, low / len(cuts), high / len(cuts))
        level = level * jnp.repeat(jnp.exp(steps), shape[axis_at] // blocks).reshape((-1,) + (1,) * (len(shape) - 1 - axis_at))
    return level


def noise(rng, dims, width, bound, shards=(), held_as=jnp.bfloat16):
    values = jax.random.normal(rng, dims, jnp.float32) * width
    if len(shards) > 0:
        values = block_scale(rng, dims, shards, -0.22, 0.18) * values
    return jnp.clip(values, min=-bound, max=bound).astype(held_as)


def setup_inputs(seed: int = 0) -> dict:
    keys = jax.random.split(jax.random.key(seed), 3)
    green = noise(keys[0], (NW, NORB, NE), 1.0, 6.0, ((0, 64),))
    chol_vecs = noise(keys[1], (NCHOL, NE, NORB), ((NCHOL * NE * NORB) ** -0.25), 0.1875, ((0, 128), (1, 2)))
    return {"green": green, "chol_vecs": chol_vecs}


def reference(green, chol_vecs):
    green_wide = green.astype(jnp.float32)

    def absorb_one(running, block):
        block_wide = block.astype(jnp.float32)
        intersection = jnp.einsum('ap,wpb->wab', block_wide, green_wide)
        intersection = lax.optimization_barrier(intersection.astype(jnp.bfloat16)).astype(jnp.float32)
        running = running - jnp.einsum('ap,wba->wpb', block_wide, intersection)
        return running, None

    gradient, unused = lax.scan(absorb_one, jnp.zeros(green.shape, jnp.float32), chol_vecs)
    return gradient
```

```python
import functools

import jax
import jax.numpy as jnp
from jax import lax
from jax.experimental import pallas as pl
from jax.experimental.pallas import tpu as pltpu
from jax.sharding import Mesh, PartitionSpec as P


STEPS = [
    {"d": ("e", "e"), "b": ("e", "e"), "c": ("e", "e"), "a": ("e", "e")},
    {"b": ("a", "e"), "a": ("b", "e"), "d": ("e", "c"), "c": ("b", "e")},
    {"a": ("e", "c"), "d": ("a", "e"), "c": ("ba", "e"), "b": ("e", "d")},
    {"b": ("e", "cd"), "c": ("ab", "e"), "a": ("ab", "e"), "d": ("ab", "e")},
    {"c": ("a", "d"), "b": ("ba", "c"), "a": ("b", "d"), "d": ("ba", "c")},
    {"c": ("ab", "d"), "b": ("aba", "e"), "d": ("aba", "e"), "a": ("ab", "c")},
    {"b": ("ba", "d"), "a": ("bab", "c"), "c": ("bab", "c"), "d": ("bab", "c")},
    {"c": ("aba", "d"), "b": ("aba", "d"), "d": ("abab", "c")},
]


def along_z(word, letter):
    if word == "e":
        return letter
    if word == "abab":
        return {"b": "aba", "a": "bab"}[letter]
    if word[-1] == letter:
        return word[:-1] or "e"
    return "abab" if word + letter == "baba" else word + letter


def along_x(word, letter):
    if word == "e":
        return letter
    if word == letter:
        return "e"
    if word == "cd":
        return "d" if letter == "c" else "c"
    return "cd"


def moved(label, letter):
    if letter in "ab":
        return along_z(label[0], letter), label[1]
    return label[0], along_x(label[1], letter)


def pairs(n, odd):
    return [(i, ((i - odd) ^ 1) + odd if odd <= i < n - odd else n - 1 - i) for i in range(n)]


def exchanged(value, letter, sizes):
    axis = "z" if letter in "ab" else "x"
    return lax.ppermute(value, axis, pairs(sizes[axis], int(letter in "bd")))


def absorb(count, *refs):
    own_ref, other_ref = refs[:2]
    halves = refs[2 : 2 + 2 * count]
    start_ref = refs[2 + 2 * count] if len(refs) > 2 * count + 3 else None
    total_ref = refs[-1]
    electrons = own_ref.shape[1]
    block = jnp.concatenate([h[...] for h in halves], axis=0)
    lefts = []
    for green in (own_ref, other_ref):
        inter = jnp.dot(block, green[...], preferred_element_type=jnp.float32).astype(jnp.bfloat16)
        lefts.append(
            jnp.concatenate([inter[m * electrons : (m + 1) * electrons] for m in range(count)], axis=1)
        )
    left = jnp.concatenate(lefts, axis=0)
    chunks, _, width = total_ref.shape
    for q in range(chunks):
        part = jnp.dot(left, block[:, q * width : (q + 1) * width], preferred_element_type=jnp.float32)
        total_ref[q] = part if start_ref is None else start_ref[q] + part


def absorbed(own, other, halves, total):
    count = len(halves) // 2
    orbitals, electrons = own.shape
    shape = (4, 2 * electrons, orbitals // 4)
    operands = [own, other, *halves] + ([] if total is None else [total])
    flops = 2 * 2 * count * 2 * electrons * electrons * orbitals
    return pl.pallas_call(
        functools.partial(absorb, count),
        out_shape=jax.ShapeDtypeStruct(shape, jnp.float32),
        in_specs=[pl.BlockSpec(memory_space=pltpu.VMEM)] * len(operands),
        out_specs=pl.BlockSpec(memory_space=pltpu.VMEM),
        input_output_aliases={} if total is None else {len(operands) - 1: 0},
        cost_estimate=pl.CostEstimate(flops=flops, bytes_accessed=4 << 20, transcendentals=0),
        compiler_params=pltpu.CompilerParams(vmem_limit_bytes=20 << 20),
    )(*operands)


def shards(sizes, green, chol_vecs):
    odd = lax.rem(lax.axis_index("x"), 2) == 1
    own = green[0]
    electrons = own.shape[1]
    half = electrons // 2
    own = jnp.where(odd, jnp.roll(own, half, axis=1), own)
    other = lax.ppermute(own, "core", [(0, 1), (1, 0)])

    cycle = []
    for x in range(0, sizes["x"], 2):
        ring = [(x, 0), (x + 1, 0), (x + 1, 1), (x, 1)]
        at = [i * 2 + e for i, e in ring]
        cycle += [(at[i], at[(i + 1) % 4]) for i in range(4)]
    first = lax.ppermute(chol_vecs[0], ("x", "elec"), cycle)

    held = {("e", "e"): first}
    total = None
    done = set()
    for step in STEPS:
        new = {moved(label, s): exchanged(held[label], s, sizes) for s, label in step.items()}
        held.update(new)
        ready = []
        for z in sorted({label[0] for label in held}):
            for one, two in (("c", "e"), ("d", "cd")):
                if (z, one) in held and (z, two) in held and (z, one) not in done:
                    done.add((z, one))
                    ready += [held[z, one], held[z, two]]
        if ready:
            total = absorbed(own, other, ready, total)

    received = lax.ppermute(total[:, electrons:], "core", [(0, 1), (1, 0)])
    here = lax.axis_index("elec") * 2 + lax.axis_index("chol")

    def chunk(r, rows):
        at = lax.bitwise_xor(here, r)
        mine = lax.dynamic_index_in_dim(total, at, 0, keepdims=False)[rows]
        return mine + lax.dynamic_index_in_dim(received, at, 0, keepdims=False)[rows]

    def to_e(v):
        return lax.ppermute(v, "elec", [(0, 1), (1, 0)])

    def to_o(v):
        return lax.ppermute(v, ("elec", "chol"), [(0, 3), (3, 0), (1, 2), (2, 1)])

    top, low = slice(0, half), slice(half, electrons)
    a = to_e(jnp.stack([chunk(2, top), chunk(1, top)]))
    b = to_o(jnp.stack([chunk(3, low), chunk(1, low)]))
    a_far = to_o(chunk(3, top) + a[1])
    b_far = to_e(chunk(2, low) + b[1])
    a_sum = chunk(0, top) + a[0] + a_far
    b_sum = chunk(0, low) + b[0] + b_far
    sum_t = jnp.where(odd, jnp.concatenate([b_sum, a_sum]), jnp.concatenate([a_sum, b_sum]))
    return -sum_t.T[None]


def solution(mesh):
    sizes = {"z": 8, "x": 4, "core": 2, "elec": 2, "chol": 2}
    fine = Mesh(mesh.devices.reshape(tuple(sizes.values())), tuple(sizes))
    walk = ("z", "x", "core")
    in_specs = (P(walk, None, None), P((*walk, "chol"), "elec", None))
    out_specs = P(walk, ("elec", "chol"), None)
    return jax.shard_map(
        functools.partial(shards, sizes), mesh=fine, in_specs=in_specs, out_specs=out_specs, check_vma=False
    )
```

```python
import functools

import jax
import jax.numpy as jnp
from jax import lax
from jax.experimental import pallas as pl
from jax.experimental.pallas import tpu as pltpu
from jax.sharding import Mesh, PartitionSpec as P


STEPS = [
    {"d": ("e", "e"), "b": ("e", "e"), "c": ("e", "e"), "a": ("e", "e")},
    {"b": ("a", "e"), "a": ("b", "e"), "d": ("e", "c"), "c": ("b", "e")},
    {"a": ("e", "c"), "d": ("a", "e"), "c": ("ba", "e"), "b": ("e", "d")},
    {"b": ("e", "cd"), "c": ("ab", "e"), "a": ("ab", "e"), "d": ("ab", "e")},
    {"c": ("a", "d"), "b": ("ba", "c"), "a": ("b", "d"), "d": ("ba", "c")},
    {"c": ("ab", "d"), "b": ("aba", "e"), "d": ("aba", "e"), "a": ("ab", "c")},
    {"b": ("ba", "d"), "a": ("bab", "c"), "c": ("bab", "c"), "d": ("bab", "c")},
    {"c": ("aba", "d"), "b": ("aba", "d"), "d": ("abab", "c")},
]


def along_z(word, letter):
    if word == "e":
        return letter
    if word == "abab":
        return {"b": "aba", "a": "bab"}[letter]
    if word[-1] == letter:
        return word[:-1] or "e"
    return "abab" if word + letter == "baba" else word + letter


def along_x(word, letter):
    if word == "e":
        return letter
    if word == letter:
        return "e"
    if word == "cd":
        return "d" if letter == "c" else "c"
    return "cd"


def moved(label, letter):
    if letter in "ab":
        return along_z(label[0], letter), label[1]
    return label[0], along_x(label[1], letter)


def pairs(n, odd):
    return [(i, ((i - odd) ^ 1) + odd if odd <= i < n - odd else n - 1 - i) for i in range(n)]


def exchanged(value, letter, sizes):
    axis = "z" if letter in "ab" else "x"
    return lax.ppermute(value, axis, pairs(sizes[axis], int(letter in "bd")))


VMEM = pl.BlockSpec(memory_space=pltpu.VMEM)
SMEM = pl.BlockSpec(memory_space=pltpu.SMEM)
PIECES = (((2, 0), (1, 0), (3, 1), (1, 1)), ((0, 0), (3, 0), (0, 1), (2, 1)))


def absorb(count, first, last, here_ref, own_ref, other_ref, *refs):
    halves = refs[: 2 * count]
    start_ref = None if first else refs[2 * count]
    outs = refs[2 * count + (0 if first else 1) :]
    electrons = own_ref.shape[1]
    half = electrons // 2
    width = own_ref.shape[0] // 4
    lefts = []
    for green in (own_ref, other_ref):
        inter = [
            jnp.dot(h[...], green[...], preferred_element_type=jnp.float32).astype(jnp.bfloat16)
            for h in halves
        ]
        lefts.append(
            jnp.concatenate(
                [jnp.concatenate(inter[2 * m : 2 * m + 2], axis=0) for m in range(count)], axis=1
            )
        )
    left = jnp.concatenate(lefts, axis=0)
    here = here_ref[0]
    for r in range(4):
        columns = pl.ds(pl.multiple_of(lax.bitwise_xor(here, r) * width, width), width)
        right = jnp.concatenate([h[:, columns] for h in halves], axis=0)
        part = jnp.dot(left, right, preferred_element_type=jnp.float32)
        value = -part if first else start_ref[r] - part
        if not last:
            outs[0][r] = value
            continue
        for group, pieces in enumerate(PIECES):
            for at, (chunk, low) in enumerate(pieces):
                if chunk == r:
                    rows = slice(low * half, (low + 1) * half)
                    outs[group][at] = value[:electrons][rows]
                    outs[2 + group][at] = value[electrons:][rows]


def absorbed(here, own, other, halves, total, last):
    count = len(halves) // 2
    orbitals, electrons = own.shape
    first = total is None
    operands = [here, own, other, *halves] + ([] if first else [total])
    if last:
        shape = [jax.ShapeDtypeStruct((4, electrons // 2, orbitals // 4), jnp.float32)] * 4
    else:
        shape = jax.ShapeDtypeStruct((4, 2 * electrons, orbitals // 4), jnp.float32)
    flops = 2 * 2 * count * 2 * electrons * electrons * orbitals
    return pl.pallas_call(
        functools.partial(absorb, count, first, last),
        out_shape=shape,
        in_specs=[SMEM] + [VMEM] * (len(operands) - 1),
        out_specs=[VMEM] * 4 if last else VMEM,
        input_output_aliases={} if first or last else {len(operands) - 1: 0},
        cost_estimate=pl.CostEstimate(flops=flops, bytes_accessed=4 << 20, transcendentals=0),
        compiler_params=pltpu.CompilerParams(vmem_limit_bytes=VLIM << 20),
    )(*operands)


def finish(odd_ref, a_ref, b_ref, a_far_ref, b_far_ref, out_ref):
    half = a_ref.shape[0]
    for place, near, far in ((0, a_ref, a_far_ref), (1, b_ref, b_far_ref)):
        columns = pl.ds(pl.multiple_of(lax.bitwise_xor(odd_ref[0], place) * half, half), half)
        out_ref[:, columns] = (near[...] + far[...]).T


def lag(core_ref, block_ref, out_ref, work_ref):
    del block_ref, out_ref

    @pl.when(core_ref[0] == 1)
    def _():
        work_ref[...] = jnp.zeros_like(work_ref)

        @pl.loop(0, LAG)
        def _(i):
            work_ref[...] = work_ref[...] * 0.5 + 1.0


def lagged(core, block):
    return pl.pallas_call(
        lag,
        out_shape=jax.ShapeDtypeStruct(block.shape, block.dtype),
        in_specs=[SMEM, pl.BlockSpec(memory_space=pl.ANY)],
        out_specs=pl.BlockSpec(memory_space=pl.ANY),
        scratch_shapes=[pltpu.VMEM((8, 128), jnp.float32)],
        input_output_aliases={1: 0},
        compiler_params=pltpu.CompilerParams(vmem_limit_bytes=1 << 20),
    )(core, block)


LAG = 0
VLIM = 8


def shards_in(sizes, green, chol_vecs):
    odd = lax.rem(lax.axis_index("x"), 2)
    own = green[0]
    electrons = own.shape[1]
    half = electrons // 2
    here = (lax.axis_index("elec") * 2 + lax.axis_index("chol")).reshape(1)

    def to_core(v):
        return lax.ppermute(v, "core", [(0, 1), (1, 0)])

    def to_e(v):
        return lax.ppermute(v, "elec", [(0, 1), (1, 0)])

    def to_o(v):
        return lax.ppermute(v, ("elec", "chol"), [(0, 3), (3, 0), (1, 2), (2, 1)])

    cycle = []
    for x in range(0, sizes["x"], 2):
        ring = [(x, 0), (x + 1, 0), (x + 1, 1), (x, 1)]
        at = [i * 2 + e for i, e in ring]
        cycle += [(at[i], at[(i + 1) % 4]) for i in range(4)]
    first = lax.ppermute(chol_vecs[0], ("x", "elec"), cycle)
    if LAG:
        first = lagged(lax.axis_index("core").reshape(1), first)
    own = jnp.where(odd == 1, jnp.roll(own, half, axis=1), own)
    other = to_core(own)
    first, other = lax.optimization_barrier((first, other))

    held = {("e", "e"): first}
    total = None
    done = set()
    for number, step in enumerate(STEPS):
        new = {}
        for s, label in step.items():
            new[moved(label, s)] = exchanged(held[label], s, sizes)
        held.update(new)
        ready = []
        for z in sorted({label[0] for label in held}):
            for one, two in (("c", "e"), ("d", "cd")):
                if (z, one) in held and (z, two) in held and (z, one) not in done:
                    done.add((z, one))
                    ready += [held[z, one], held[z, two]]
        if ready:
            total = absorbed(here, own, other, ready, total, number == len(STEPS) - 1)

    keep_1, keep_2, give_1, give_2 = total
    sum_1 = keep_1 + to_core(give_1)
    sum_2 = keep_2 + to_core(give_2)
    a, b = to_e(sum_1[:2]), to_o(sum_1[2:])
    a_far = to_o(sum_2[1] + a[1])
    b_far = to_e(sum_2[3] + b[1])
    out = pl.pallas_call(
        finish,
        out_shape=jax.ShapeDtypeStruct((green.shape[1] // 4, electrons), jnp.float32),
        in_specs=[SMEM] + [VMEM] * 4,
        out_specs=VMEM,
        compiler_params=pltpu.CompilerParams(vmem_limit_bytes=4 << 20),
    )(odd.reshape(1), sum_2[0] + a[0], sum_2[2] + b[0], a_far, b_far)
    return out[None]


def solution(mesh):
    sizes = {"z": 8, "x": 4, "core": 2, "elec": 2, "chol": 2}
    fine = Mesh(mesh.devices.reshape(tuple(sizes.values())), tuple(sizes))
    walk = ("z", "x", "core")
    in_specs = (P(walk, None, None), P((*walk, "chol"), "elec", None))
    out_specs = P(walk, ("elec", "chol"), None)
    return jax.shard_map(
        functools.partial(shards_in, sizes), mesh=fine, in_specs=in_specs, out_specs=out_specs, check_vma=False
    )
```

```python
import functools

import jax
import jax.numpy as jnp
from jax import lax
from jax.experimental import pallas as pl
from jax.experimental.pallas import tpu as pltpu
from jax.sharding import Mesh, PartitionSpec as P


STEPS = [
    {"d": ("e", "e"), "b": ("e", "e"), "c": ("e", "e"), "a": ("e", "e")},
    {"b": ("a", "e"), "a": ("b", "e"), "d": ("e", "c"), "c": ("b", "e")},
    {"a": ("e", "c"), "d": ("a", "e"), "c": ("ba", "e"), "b": ("e", "d")},
    {"b": ("e", "cd"), "c": ("ab", "e"), "a": ("ab", "e"), "d": ("ab", "e")},
    {"c": ("a", "d"), "b": ("ba", "c"), "a": ("b", "d"), "d": ("ba", "c")},
    {"c": ("ab", "d"), "b": ("aba", "e"), "d": ("aba", "e"), "a": ("ab", "c")},
    {"b": ("ba", "d"), "a": ("bab", "c"), "c": ("bab", "c"), "d": ("bab", "c")},
    {"c": ("aba", "d"), "b": ("aba", "d"), "d": ("abab", "c")},
]


def along_z(word, letter):
    if word == "e":
        return letter
    if word == "abab":
        return {"b": "aba", "a": "bab"}[letter]
    if word[-1] == letter:
        return word[:-1] or "e"
    return "abab" if word + letter == "baba" else word + letter


def along_x(word, letter):
    if word == "e":
        return letter
    if word == letter:
        return "e"
    if word == "cd":
        return "d" if letter == "c" else "c"
    return "cd"


def moved(label, letter):
    if letter in "ab":
        return along_z(label[0], letter), label[1]
    return label[0], along_x(label[1], letter)


def pairs(n, odd):
    return [(i, ((i - odd) ^ 1) + odd if odd <= i < n - odd else n - 1 - i) for i in range(n)]


def exchanged(value, letter, sizes):
    axis = "z" if letter in "ab" else "x"
    return lax.ppermute(value, axis, pairs(sizes[axis], int(letter in "bd")))


VMEM = pl.BlockSpec(memory_space=pltpu.VMEM)
SMEM = pl.BlockSpec(memory_space=pltpu.SMEM)
PIECES = (((2, 0), (1, 0), (3, 1), (1, 1)), ((0, 0), (3, 0), (0, 1), (2, 1)))


def absorb(count, first, last, here_ref, own_ref, other_ref, *refs):
    halves = refs[: 2 * count]
    start_ref = None if first else refs[2 * count]
    outs = refs[2 * count + (0 if first else 1) :]
    electrons = own_ref.shape[1]
    half = electrons // 2
    width = own_ref.shape[0] // 4
    lefts = []
    for green in (own_ref, other_ref):
        inter = [
            jnp.dot(h[...], green[...], preferred_element_type=jnp.float32).astype(jnp.bfloat16)
            for h in halves
        ]
        lefts.append(
            jnp.concatenate(
                [jnp.concatenate(inter[2 * m : 2 * m + 2], axis=0) for m in range(count)], axis=1
            )
        )
    left = jnp.concatenate(lefts, axis=0)
    here = here_ref[0]
    for r in range(4):
        columns = pl.ds(pl.multiple_of(lax.bitwise_xor(here, r) * width, width), width)
        right = jnp.concatenate([h[:, columns] for h in halves], axis=0)
        part = jnp.dot(left, right, preferred_element_type=jnp.float32)
        value = -part if first else start_ref[r] - part
        if not last:
            outs[0][r] = value
            continue
        for group, pieces in enumerate(PIECES):
            for at, (chunk, low) in enumerate(pieces):
                if chunk == r:
                    rows = slice(low * half, (low + 1) * half)
                    outs[group][at] = value[:electrons][rows]
                    outs[2 + group][at] = value[electrons:][rows]


def absorbed(here, own, other, halves, total, last):
    count = len(halves) // 2
    orbitals, electrons = own.shape
    first = total is None
    operands = [here, own, other, *halves] + ([] if first else [total])
    if last:
        shape = [jax.ShapeDtypeStruct((4, electrons // 2, orbitals // 4), jnp.float32)] * 4
    else:
        shape = jax.ShapeDtypeStruct((4, 2 * electrons, orbitals // 4), jnp.float32)
    flops = 2 * 2 * count * 2 * electrons * electrons * orbitals
    return pl.pallas_call(
        functools.partial(absorb, count, first, last),
        out_shape=shape,
        in_specs=[SMEM] + [VMEM] * (len(operands) - 1),
        out_specs=[VMEM] * 4 if last else VMEM,
        input_output_aliases={} if first or last else {len(operands) - 1: 0},
        cost_estimate=pl.CostEstimate(flops=flops, bytes_accessed=4 << 20, transcendentals=0),
        compiler_params=pltpu.CompilerParams(vmem_limit_bytes=VLIM << 20),
    )(*operands)


def finish(odd_ref, a_ref, b_ref, a_far_ref, b_far_ref, out_ref):
    half = a_ref.shape[0]
    for place, near, far in ((0, a_ref, a_far_ref), (1, b_ref, b_far_ref)):
        columns = pl.ds(pl.multiple_of(lax.bitwise_xor(odd_ref[0], place) * half, half), half)
        out_ref[:, columns] = (near[...] + far[...]).T


def lag(core_ref, block_ref, out_ref, work_ref):
    del block_ref, out_ref

    @pl.when(core_ref[0] == 1)
    def _():
        work_ref[...] = jnp.zeros_like(work_ref)

        @pl.loop(0, LAG)
        def _(i):
            work_ref[...] = work_ref[...] * 0.5 + 1.0


def lagged(core, block):
    return pl.pallas_call(
        lag,
        out_shape=jax.ShapeDtypeStruct(block.shape, block.dtype),
        in_specs=[SMEM, pl.BlockSpec(memory_space=pl.ANY)],
        out_specs=pl.BlockSpec(memory_space=pl.ANY),
        scratch_shapes=[pltpu.VMEM((8, 128), jnp.float32)],
        input_output_aliases={1: 0},
        compiler_params=pltpu.CompilerParams(vmem_limit_bytes=1 << 20),
    )(core, block)


LAG = 0
VLIM = 8


def shards_in(sizes, green, chol_vecs):
    odd = lax.rem(lax.axis_index("x"), 2)
    own = green[0]
    electrons = own.shape[1]
    half = electrons // 2
    here = (lax.axis_index("elec") * 2 + lax.axis_index("chol")).reshape(1)

    def to_core(v):
        return lax.ppermute(v, "core", [(0, 1), (1, 0)])

    def to_e(v):
        return lax.ppermute(v, "elec", [(0, 1), (1, 0)])

    def to_o(v):
        return lax.ppermute(v, ("elec", "chol"), [(0, 3), (3, 0), (1, 2), (2, 1)])

    cycle = []
    for x in range(0, sizes["x"], 2):
        ring = [(x, 0), (x + 1, 0), (x + 1, 1), (x, 1)]
        at = [i * 2 + e for i, e in ring]
        cycle += [(at[i], at[(i + 1) % 4]) for i in range(4)]
    first = lax.ppermute(chol_vecs[0], ("x", "elec"), cycle)
    if LAG:
        first = lagged(lax.axis_index("core").reshape(1), first)
    own = jnp.where(odd == 1, jnp.roll(own, half, axis=1), own)
    other = to_core(own)
    first, other = lax.optimization_barrier((first, other))

    held = {("e", "e"): first}
    total = None
    done = set()
    for number, step in enumerate(STEPS):
        new = {}
        for s, label in step.items():
            new[moved(label, s)] = exchanged(held[label], s, sizes)
        held.update(new)
        ready = []
        for z in sorted({label[0] for label in held}):
            for one, two in (("c", "e"), ("d", "cd")):
                if (z, one) in held and (z, two) in held and (z, one) not in done:
                    done.add((z, one))
                    ready += [held[z, one], held[z, two]]
        if ready:
            total = absorbed(here, own, other, ready, total, number == len(STEPS) - 1)

    keep_1, keep_2, give_1, give_2 = total
    sum_1 = keep_1 + to_core(give_1)
    sum_2 = keep_2 + to_core(give_2)
    near = sum_1.astype(jnp.bfloat16)
    a, b = to_e(near[:2]), to_o(near[2:])
    a_far = to_o((sum_2[1] + a[1]).astype(jnp.bfloat16))
    b_far = to_e((sum_2[3] + b[1]).astype(jnp.bfloat16))
    out = pl.pallas_call(
        finish,
        out_shape=jax.ShapeDtypeStruct((green.shape[1] // 4, electrons), jnp.float32),
        in_specs=[SMEM] + [VMEM] * 4,
        out_specs=VMEM,
        compiler_params=pltpu.CompilerParams(vmem_limit_bytes=4 << 20),
    )(odd.reshape(1), sum_2[0] + a[0], sum_2[2] + b[0], a_far, b_far)
    return out[None]


def solution(mesh):
    sizes = {"z": 8, "x": 4, "core": 2, "elec": 2, "chol": 2}
    fine = Mesh(mesh.devices.reshape(tuple(sizes.values())), tuple(sizes))
    walk = ("z", "x", "core")
    in_specs = (P(walk, None, None), P((*walk, "chol"), "elec", None))
    out_specs = P(walk, ("elec", "chol"), None)
    return jax.shard_map(
        functools.partial(shards_in, sizes), mesh=fine, in_specs=in_specs, out_specs=out_specs, check_vma=False
    )
```
